32 devices in a mesh: group: 2 (over x), row: 16 (over z, y, core).
Axes of the slice: x: 2, y: 2, z: 4, core: 2. Of those that a mesh axis runs over, the one named last changes fastest.
Arguments:
- sources: float32 [4, 16, 8192], P('group', None, 'row'), parts along dimension 0, may hold values from -6 to 6
- lower_sources: float32 [4, 16, 8192], P('group', None, 'row'), parts along dimension 0, may hold values from -6 to 6
- upper_operator: float32 [16384, 8192], P(('group', 'row')), parts along dimension 0, may hold values from -0.0625 to 0.0625
- lower_operator: float32 [16384, 8192], P(('group', 'row')), parts along dimension 0, may hold values from -0.0625 to 0.0625
- upper_impedance: float32 [16384], P(('group', 'row')), parts along dimension 0, may hold values from 0.5 to 2
- lower_impedance: float32 [16384], P(('group', 'row')), parts along dimension 0, may hold values from 0.5 to 2
Outputs:
- lower_field: float32 [4, 16, 8192], P('group', None, 'row'), parts along dimension 0
- reflected: float32 [4, 16, 8192], P('group', None, 'row'), parts along dimension 0
The draws below stay inside these ranges and needn't reach their ends.
There are 2 independent parts, one for each index of `group`. The reference program is written for one: setup_inputs(seed, part) draws one part's arguments, and reference() takes and returns one part's arrays. A program takes and returns all parts, laid end to end along the dimension named above; each array names one. Nothing has to cross between parts.
All inputs are finite; a program needn't handle non-finite values.
Results may differ from the reference program's by a relative error of at most 0.000098.
Values sent between devices are 32-bit elements; how exact they have to be, the bound alone decides.
No kernel may reach another device: no remote copies, remote signals or barrier semaphores. Data moves between devices by JAX's collectives and lax.ppermute only.
A program may use at most 64 MiB of HBM per device.

```python
import math
import jax
import jax.numpy as jnp
from jax import lax

N = 8192
COLS = 16
BATCHES = 2


def level_of(key, extent, cuts, smallest, largest):
    gain, own = 1.0, jax.random.fold_in(key, 6)
    for dim, shards_of in cuts:
        heights = jnp.exp(jax.random.uniform(jax.random.fold_in(own, dim), (shards_of,), jnp.float32, smallest / len(cuts), largest / len(cuts)))
        gain = gain * jnp.repeat(heights, extent[dim] // shards_of).reshape([-1 if axis == dim else 1 for axis in range(len(extent))])
    return gain


def gaussian(stream_key, shape, scale, reach, cuts=(), kind=jnp.bfloat16):
    gain = level_of(stream_key, shape, cuts, -0.22, 0.18) if cuts else 1.0
    result = jax.random.normal(stream_key, shape, jnp.float32) * scale * gain
    return jnp.minimum(jnp.maximum(result, -reach), reach).astype(kind)


def setup_inputs(seed: int = 0, part: int = 0) -> dict:
    seeds = jax.random.split(jax.random.key(seed), 7)
    part_keys = jax.random.split(jax.random.fold_in(seeds[6], part), 7)
    return {
        "sources": gaussian(part_keys[0], (BATCHES, COLS, N), 1.0, 6.0, ((2, 16),), jnp.float32),
        "lower_sources": gaussian(part_keys[1], (BATCHES, COLS, N), 1.0, 6.0, ((2, 16),), jnp.float32),
        "upper_operator": gaussian(part_keys[2], (N, N), N ** -0.5, 0.0625, ((0, 16),), jnp.float32),
        "lower_operator": gaussian(part_keys[3], (N, N), N ** -0.5, 0.0625, ((0, 16),), jnp.float32),
        "upper_impedance": jnp.clip(jnp.exp(math.log(2.0) - 1.3862944 * jax.random.uniform(part_keys[4], (N,), jnp.float32) ** level_of(part_keys[4], (N,), ((0, 16),), -0.2, 0.2)), 0.5, 2.0),
        "lower_impedance": jnp.clip(jnp.exp(math.log(2.0) - 1.3862944 * jax.random.uniform(part_keys[5], (N,), jnp.float32) ** level_of(part_keys[5], (N,), ((0, 16),), -0.2, 0.2)), 0.5, 2.0),
    }


def reference(sources, lower_sources, upper_operator, lower_operator, upper_impedance, lower_impedance):
    highest = lax.Precision.HIGHEST
    downward = jnp.einsum("bcj,ij->bci", sources, upper_operator, precision=highest)
    lower_field = jnp.einsum("bcj,ij->bci", downward, lower_operator, precision=highest)
    scaled = lower_impedance * lower_field + lower_sources
    bounced = jnp.einsum("bci,ij->bcj", scaled, lower_operator, precision=highest)
    mixed = upper_impedance * bounced - downward
    reflected = jnp.einsum("bci,ij->bcj", mixed, upper_operator, precision=highest)
    return lower_field, reflected
```

```python
import functools

import jax
import jax.numpy as jnp
from jax import lax
from jax.experimental import pallas as pl
from jax.experimental.pallas import tpu as pltpu
from jax.sharding import PartitionSpec as P


F32, BF16 = jnp.float32, jnp.bfloat16
VMEM = pl.BlockSpec(memory_space=pltpu.VMEM)
PARAMS = pltpu.CompilerParams(vmem_limit_bytes=8 << 20)


def halves(x):
    high = x.astype(BF16)
    return high, (x - high.astype(F32)).astype(BF16)


def dot(x, w, dims):
    return lax.dot_general(x, w, (dims, ((), ())), preferred_element_type=F32)


def product(x, high, low, dims):
    x_high, x_low = halves(x)
    rows = x.shape[0]
    both = dot(jnp.concatenate([x_high, x_low], axis=0), high, dims)
    return both[:rows] + both[rows:] + dot(x_high, low, dims)


def kernel_call(body, operands, out_shapes, dots):
    out = [jax.ShapeDtypeStruct(s, F32) for s in out_shapes]
    rows, width = operands[0].shape[-2:]
    return pl.pallas_call(
        body,
        in_specs=[VMEM] * len(operands),
        out_specs=[VMEM] * len(out),
        out_shape=out,
        compiler_params=PARAMS,
        cost_estimate=pl.CostEstimate(
            flops=dots * 6 * rows * width * width, bytes_accessed=dots * 4 * width * width, transcendentals=0
        ),
    )(*operands)


def split(operator):
    rows, columns = operator.shape
    step = min(64, rows)

    def body(w_ref, high_ref, low_ref):
        at = pl.ds(pl.multiple_of(pl.program_id(0) * step, step), step)
        high_ref[at, :], low_ref[at, :] = halves(w_ref[...])

    return pl.pallas_call(
        body,
        grid=(rows // step,),
        in_specs=[pl.BlockSpec((step, columns), lambda i: (i, 0))],
        out_specs=[VMEM, VMEM],
        out_shape=[pltpu.VMEM((rows, columns), BF16)] * 2,
        compiler_params=PARAMS,
        cost_estimate=pl.CostEstimate(flops=4 * rows * columns, bytes_accessed=8 * rows * columns, transcendentals=0),
    )(pltpu.with_memory_space_constraint(operator, pltpu.HBM))


class Ring:
    def __init__(self, n):
        self.n = n
        bits = [1 << b for b in range(1, n.bit_length() - 1)]
        self.near, self.side, self.far = bits[0], bits[1], bits[:1:-1]
        held = [0]
        for k in self.far:
            held = held + [o ^ k for o in held]
        self.held = held
        self.early = held + [self.near]
        self.late = (
            [o ^ self.side for o in held] + [o ^ self.side ^ self.near for o in held] + [o ^ self.near for o in held[1:]]
        )

    def swap(self, v, k):
        return lax.ppermute(v, "row", [(i, i ^ k) for i in range(self.n)])


def at_owner(offset, width):
    owner = jnp.bitwise_xor(lax.axis_index("row"), offset)
    return pl.ds(pl.multiple_of(owner * width, width), width)


def forward(ring, v, parts, tail=None):
    rows, width = v.shape
    held = v[None]
    for k in ring.far:
        held = jnp.concatenate([held, ring.swap(held, k)])
    near = ring.swap(v, ring.near)[None]
    side = ring.swap(held, ring.side)
    diagonal = ring.swap(held, ring.side ^ ring.near)
    rest = ring.swap(held[1:], ring.near)
    early = jnp.concatenate([held, near])
    early_partner = ring.swap(early, 1)
    late = jnp.concatenate([side, diagonal, rest])
    late_partner = ring.swap(late, 1)

    def term(pieces_ref, offsets, high_ref, low_ref):
        total = None
        for p, offset in enumerate(offsets):
            at = at_owner(offset, width)
            new = product(pieces_ref[p], high_ref[:, at], low_ref[:, at], ((1,), (1,)))
            total = new if total is None else total + new
        return total

    partner = lambda offsets: [o ^ 1 for o in offsets]

    def first(e_ref, ep_ref, high_ref, low_ref, out_ref):
        out_ref[...] = term(e_ref, ring.early, high_ref, low_ref) + term(ep_ref, partner(ring.early), high_ref, low_ref)

    def second(l_ref, a_ref, high_ref, low_ref, out_ref):
        out_ref[...] = a_ref[...] + term(l_ref, ring.late, high_ref, low_ref)

    def third(lp_ref, a_ref, high_ref, low_ref, *refs):
        out = a_ref[...] + term(lp_ref, partner(ring.late), high_ref, low_ref)
        if tail is None:
            refs[0][...] = out
        else:
            tail[0](out, high_ref, low_ref, *refs)

    a = kernel_call(first, [early, early_partner, *parts], [(rows, width)], 2 * len(ring.early))[0]
    a = kernel_call(second, [late, a, *parts], [(rows, width)], len(ring.late))[0]
    extra, shapes, dots = ([], [(rows, width)], 0) if tail is None else tail[1:]
    return kernel_call(third, [late_partner, a, *parts, *extra], shapes, len(ring.late) + dots)


def blocks(x, offsets, high_ref, low_ref, out_ref):
    for p, offset in enumerate(offsets):
        at = at_owner(offset, x.shape[1])
        out_ref[p] = product(x, high_ref[:, at], low_ref[:, at], ((1,), (0,)))


def backward(ring, v, parts, outgoing):
    rows, width = v.shape
    shape = lambda offsets: (len(offsets), rows, width)

    def body(offsets, v_ref, high_ref, low_ref, out_ref):
        blocks(v_ref[...], offsets, high_ref, low_ref, out_ref)

    def call(offsets):
        return kernel_call(functools.partial(body, offsets), [v, *parts], [shape(offsets)], len(offsets))[0]

    h = len(ring.held)
    late = call(ring.late) + ring.swap(outgoing, 1)
    side = ring.swap(late[:h], ring.side)
    diagonal = ring.swap(late[h : 2 * h], ring.side ^ ring.near)
    rest = ring.swap(late[2 * h :], ring.near)
    partner = ring.swap(call([o ^ 1 for o in ring.early]), 1)
    early = call(ring.early) + partner
    near = ring.swap(early[h], ring.near)
    held = early[:h] + side + diagonal
    held = jnp.concatenate([held[:1], held[1:] + rest])
    for k in ring.far[::-1]:
        half = held.shape[0] // 2
        last = ring.swap(held[half:], k)
        if half == 1:
            return held[0], last[0], near
        held = held[:half] + last


def body(n, sources, lower_sources, upper, lower, upper_impedance, lower_impedance):
    ring = Ring(n)
    shape = sources.shape
    width = shape[-1]
    entering = sources.reshape(-1, width)
    inside = lower_sources.reshape(-1, width)
    rows = entering.shape[0]
    late_partner = [o ^ 1 for o in ring.late]
    late_shape = (len(ring.late), rows, width)
    upper_parts, lower_parts = split(upper), split(lower)

    (downward,) = forward(ring, entering, upper_parts)

    def scale(out, high_ref, low_ref, z_ref, inside_ref, field_ref, scaled_ref, blocks_ref):
        field_ref[...] = out
        scaled = z_ref[...] * out + inside_ref[...]
        scaled_ref[...] = scaled
        blocks(scaled, late_partner, high_ref, low_ref, blocks_ref)

    lower_field, scaled, outgoing = forward(
        ring,
        downward,
        lower_parts,
        (scale, [lower_impedance[None], inside], [(rows, width)] * 2 + [late_shape], len(late_partner)),
    )
    terms = backward(ring, scaled, lower_parts, outgoing)

    def mix(a_ref, b_ref, c_ref, high_ref, low_ref, z_ref, down_ref, mixed_ref, blocks_ref):
        mixed = z_ref[...] * (a_ref[...] + b_ref[...] + c_ref[...]) - down_ref[...]
        mixed_ref[...] = mixed
        blocks(mixed, late_partner, high_ref, low_ref, blocks_ref)

    mixed, outgoing = kernel_call(
        mix,
        [*terms, *upper_parts, upper_impedance[None], downward],
        [(rows, width), late_shape],
        len(late_partner),
    )
    a, b, c = backward(ring, mixed, upper_parts, outgoing)
    return lower_field.reshape(shape), (a + b + c).reshape(shape)


def solution(mesh):
    traces, operator, points = P("group", None, "row"), P(("group", "row"), None), P(("group", "row"))
    return jax.shard_map(
        functools.partial(body, mesh.shape["row"]),
        mesh=mesh,
        in_specs=(traces, traces, operator, operator, points, points),
        out_specs=(traces, traces),
        check_vma=False,
    )
```
